32 devices in a mesh: beam: 2 (over x), band: 2 (over core), tm: 8 (over z, y).
Axes of the slice: x: 2, y: 2, z: 4, core: 2. Of those that a mesh axis runs over, the one named last changes fastest.
Arguments:
- samples: bfloat16 [2048, 32768], P(('beam', 'band'), 'tm'), parts along dimension 0, may hold values from -3 to 3
- clip_mask: int32 [2048, 256], P(('beam', 'band'), 'tm'), parts along dimension 0, may hold values 0 or 1
- delays: int32 [8, 1024], P(None, 'band'), may hold values from 0 to 4095
- templates: bfloat16 [2, 64, 1024], replicated, may hold values from -0.125 to 0.125
Outputs:
- powers: float32 [16, 64, 16384], P(('beam', 'tm'), None, 'band'), parts along dimension 0
The draws below stay inside these ranges and needn't reach their ends.
There are 2 independent parts, one for each index of `beam`. The reference program is written for one: setup_inputs(seed, part) draws one part's arguments, and reference() takes and returns one part's arrays. A program takes and returns all parts, laid end to end along the dimension named above; an argument that names none is the same for every part. Nothing has to cross between parts.
All inputs are finite; a program needn't handle non-finite values. No bound on the sum of `clip_mask` on one device may be relied on, other than what follows from the above.
Results may differ from the reference program's by a relative error of at most 0.0095.
Values may be sent and summed in bfloat16 or wider, within the bound.
A program may use at most 192 MiB of HBM per device.

```python
import math
import jax
import jax.numpy as jnp
from jax import lax

CHANNELS = 1024
FFT_LEN = 8192
TEMPLATES = 64
TEMPLATE_LEN = 1024
FLAG_SPAN = 128
SEARCH = 16384
SLAB = 4096
SAMPLES = 32768
DMS = 8
N_TM = 8


def draw_samples(key, part):
    noise_key = jax.random.fold_in(key, 11)
    step_key = jax.random.fold_in(key, 12)
    offset_key = jax.random.fold_in(key, 13)
    lowest_step = 15 * FFT_LEN // 100
    highest_step = 48 * FFT_LEN // 100
    tone_steps = jax.random.randint(step_key, (CHANNELS, 1), lowest_step, highest_step, dtype=jnp.int32)
    offsets = jax.random.randint(offset_key, (CHANNELS, 1), 0, FFT_LEN, dtype=jnp.int32)
    sample_index = jnp.arange(SAMPLES, dtype=jnp.int32) % FFT_LEN
    turn_count = (sample_index[None, :] * tone_steps + offsets) % FFT_LEN
    angles = turn_count.astype(jnp.float32) * (2.0 * math.pi / FFT_LEN)
    tone_wave = jnp.sin(angles)
    noise_part = 0.2 * jax.random.truncated_normal(noise_key, -3.0, 3.0, (CHANNELS, SAMPLES), jnp.float32)
    amplitude = 2.0
    return (amplitude * tone_wave + noise_part).astype(jnp.bfloat16)


def place_ends(values, key, smallest, high):
    place = [jax.random.randint(jax.random.fold_in(key, axis), (), 0, length) for axis, length in enumerate(values.shape)]
    main_axis = values.shape.index(max(values.shape))
    beside = place[:main_axis] + [(place[main_axis] + 1) % values.shape[main_axis]] + place[main_axis + 1:]
    return values.at[tuple(place)].set(smallest).at[tuple(beside)].set(high)


def noise(key, extent, deviation, most, kind=jnp.bfloat16):
    entries = deviation * jax.random.normal(key, extent, jnp.float32)
    return jnp.clip(entries, min=-most, max=most).astype(kind)


def setup_inputs(seed: int = 0, part: int = 0) -> dict:
    arg_keys = jax.random.split(jax.random.key(seed), 5)
    part_keys = jax.random.split(jax.random.fold_in(arg_keys[4], part), 5)
    return {
        "samples": draw_samples(jax.random.fold_in(jax.random.fold_in(arg_keys[4], part), 71), part),
        "clip_mask": place_ends((jax.random.randint(part_keys[1], (CHANNELS, SAMPLES // FLAG_SPAN), 0, 8) < 7).astype(jnp.int32), jax.random.fold_in(part_keys[1], 1), 0, 1),
        "delays": place_ends(jax.random.randint(arg_keys[2], (DMS, CHANNELS), 0, SLAB), jax.random.fold_in(arg_keys[2], 1), 0, SLAB - 1).astype(jnp.int32),
        "templates": noise(arg_keys[3], (2, TEMPLATES, TEMPLATE_LEN), (2 * TEMPLATE_LEN) ** -0.5, 0.125),
    }


clip_level = 2.5
highest = lax.Precision.HIGHEST

def reference(samples, clip_mask, delays, templates):
    widened = jnp.repeat(clip_mask, FLAG_SPAN, axis=1).astype(jnp.float32)
    cleaned = (jnp.clip(samples.astype(jnp.float32), -clip_level, clip_level) * widened).astype(jnp.bfloat16)
    slab_rows = cleaned.reshape(CHANNELS, N_TM, SLAB).transpose(1, 0, 2)

    def slab_spectrum(slab_data):
        spectrum = jnp.fft.rfft(slab_data.astype(jnp.float32), n=FFT_LEN, axis=-1)[:, :SLAB]
        return (jnp.real(spectrum).astype(jnp.bfloat16), jnp.imag(spectrum).astype(jnp.bfloat16))
    spec_real, spec_imag = lax.map(slab_spectrum, slab_rows)
    bin_width = min(256, SLAB)
    bin_groups = SLAB // bin_width
    real_groups = spec_real.reshape(N_TM, CHANNELS, bin_groups, bin_width).transpose(2, 0, 1, 3)
    imag_groups = spec_imag.reshape(N_TM, CHANNELS, bin_groups, bin_width).transpose(2, 0, 1, 3)
    group_starts = jnp.arange(bin_groups, dtype=jnp.int32) * bin_width

    def rotate(pieces):
        real_piece, imag_piece, first_bin = pieces
        bin_index = first_bin + jnp.arange(bin_width, dtype=jnp.int32)
        turn_count = delays[:, :, None] * bin_index[None, None, :] % FFT_LEN
        angles = turn_count.astype(jnp.float32) * (2.0 * math.pi / FFT_LEN)
        cos_part = jnp.cos(angles)
        sin_part = jnp.sin(angles)
        real_data = real_piece.astype(jnp.float32)
        imag_data = imag_piece.astype(jnp.float32)
        pattern = 'dck,sck->sdk'
        out_real = jnp.einsum(pattern, cos_part, real_data, precision=highest) + jnp.einsum(pattern, sin_part, imag_data, precision=highest)
        out_imag = jnp.einsum(pattern, cos_part, imag_data, precision=highest) - jnp.einsum(pattern, sin_part, real_data, precision=highest)
        return (out_real, out_imag)
    rot_real, rot_imag = lax.map(rotate, (real_groups, imag_groups, group_starts))
    scale_dm = 1.0 / math.sqrt(CHANNELS)
    rot_real = rot_real.transpose(1, 2, 0, 3).reshape(N_TM, DMS, SLAB) * scale_dm
    rot_imag = rot_imag.transpose(1, 2, 0, 3).reshape(N_TM, DMS, SLAB) * scale_dm
    nyquist = jnp.zeros((N_TM, DMS, 1), jnp.float32)
    combined = lax.complex(jnp.concatenate([rot_real, nyquist], axis=2), jnp.concatenate([rot_imag, nyquist], axis=2))
    padded_out = jnp.fft.irfft(combined, n=FFT_LEN, axis=-1)
    own_part = padded_out[:, :, :SLAB]
    tail_part = padded_out[:, :, SLAB:]
    carried = jnp.concatenate([jnp.zeros((1, DMS, SLAB), padded_out.dtype), tail_part[:-1]], axis=0)
    series = (own_part + carried).transpose(1, 0, 2).reshape(DMS, SAMPLES)
    spectrum = jnp.fft.fft(series, axis=-1)[:, :SEARCH] / math.sqrt(SAMPLES)
    bins_real = lax.optimization_barrier(jnp.real(spectrum).astype(jnp.bfloat16)).astype(jnp.float32)
    bins_imag = lax.optimization_barrier(jnp.imag(spectrum).astype(jnp.bfloat16)).astype(jnp.float32)
    half_taps = TEMPLATE_LEN // 2
    frame_len = SEARCH + TEMPLATE_LEN
    framed = lax.complex(jnp.pad(bins_real, ((0, 0), (half_taps, half_taps))), jnp.pad(bins_imag, ((0, 0), (half_taps, half_taps))))
    kernel = lax.complex(templates[0].astype(jnp.float32), templates[1].astype(jnp.float32))
    reversed_taps = jnp.concatenate([kernel[:, :1], jnp.zeros((TEMPLATES, frame_len - TEMPLATE_LEN), kernel.dtype), kernel[:, :0:-1]], axis=1)
    kernel_spec = jnp.fft.fft(reversed_taps, axis=-1)

    def correlate(frame_row):
        product = jnp.fft.ifft(jnp.fft.fft(frame_row)[None, :] * kernel_spec, axis=-1)[:, :SEARCH]
        return jnp.square(jnp.real(product)) + jnp.square(jnp.imag(product))
    return lax.map(correlate, framed)
```

```python
import math

import jax
import jax.numpy as jnp
from jax import lax
from jax.experimental import pallas as pl
from jax.experimental.pallas import tpu as pltpu
from jax.sharding import PartitionSpec as P

CHANNELS = 1024
SEARCH = 16384
LANES = 128

clip_level = 2.5
fine = lax.Precision.HIGH


def counting(length):
    return jnp.arange(length, dtype=jnp.int32)


def phase_table(first_index, second_index, period):
    turn_count = first_index[:, None] * second_index[None, :] % period
    angles = turn_count.astype(jnp.float32) * (2.0 * math.pi / period)
    return (jnp.cos(angles), jnp.sin(angles))


def dedisperse(samples, clip_mask, delays):
    chan_count, slab_len = samples.shape
    rows = slab_len // LANES
    dm_count = delays.shape[0]
    tm_count = lax.axis_size("tm")
    band_count = lax.axis_size("band")
    padded_len = 2 * slab_len
    scale = 1.0 / math.sqrt(CHANNELS)
    assert clip_mask.shape[1] == rows and dm_count == tm_count
    mesh_ids = pl.DeviceIdType.MESH
    lane_bits = LANES.bit_length() - 1
    pitch = rows + 8
    width = 2 * LANES
    chunks = slab_len // width
    group = width // rows
    block = 64
    spans = chan_count // LANES
    padded_rows = 2 * rows

    def kernel(
        delay_ref, lag_ref, sample_ref, mask_ref, out_ref,
        held_in, natural, same_ref, before_ref, flag_ref, lag_rows, carry_ref, part_ref, held_ref,
        load_sem, sent, arrived,
    ):
        me = lax.axis_index("tm")
        band = lax.axis_index("band")

        def load(j):
            start = pl.multiple_of(j * width, width)
            cut = pl.ds(start, width)
            return pltpu.make_async_copy(sample_ref.at[:, cut], held_in.at[:, cut], load_sem.at[j])

        for j in range(chunks):
            load(j).start()

        barrier = pltpu.get_barrier_semaphore()
        peers = tm_count * band_count - 1
        place = me * band_count + band

        def greet(k, _):
            other = lax.rem(place + k, peers + 1)
            pl.semaphore_signal(
                barrier, 1,
                device_id={"tm": other // band_count, "band": lax.rem(other, band_count)},
                device_id_type=mesh_ids,
            )
            return 0

        lax.fori_loop(1, peers + 1, greet, 0)

        flag_ref[...] = mask_ref[...].astype(jnp.float32).T.astype(jnp.bfloat16)
        spread_lane = lax.broadcasted_iota(jnp.int32, (LANES, rows * LANES), 1)
        spread_row = lax.broadcasted_iota(jnp.int32, (LANES, rows * LANES), 0)
        spread = (spread_lane // rows == spread_row).astype(jnp.float32).astype(jnp.bfloat16)
        row_lags = (lag_ref[...] >> lane_bits).astype(jnp.float32).astype(jnp.bfloat16)
        for i in range(spans):
            lag_rows[i] = jnp.dot(
                row_lags[:, i * LANES : (i + 1) * LANES], spread, preferred_element_type=jnp.float32
            )

        def take(j, _):
            load(j).wait()
            start = pl.multiple_of(j * width, width)
            first = lax.broadcasted_iota(jnp.int32, (rows, width), 0) - 2 * j
            which = lax.broadcasted_iota(jnp.int32, (rows, width), 1) // LANES
            pick = (first == which).astype(jnp.float32).astype(jnp.bfloat16)
            flags = jnp.dot(flag_ref[...], pick, preferred_element_type=jnp.float32)
            for g in range(chan_count // 16):
                values = held_in[16 * g : 16 * g + 16, pl.ds(start, width)]
                values = jnp.clip(values, -clip_level, clip_level).astype(jnp.float32)
                values = values * flags[16 * g : 16 * g + 16]
                for h in range(2):
                    for t in range(2):
                        natural[pl.ds((16 * g + 8 * t) * pitch + 8 + 2 * j + h, 8, stride=pitch), :] = (
                            values[8 * t : 8 * t + 8, h * LANES : (h + 1) * LANES]
                        )
            return 0

        lax.fori_loop(0, chunks, take, 0)

        def pack(i, _):
            base = pl.multiple_of(i * (8 * pitch), 8)
            last = natural[pl.ds(base + pitch - 1, 8, stride=pitch), :]
            natural[pl.ds(base + 7, 8, stride=pitch), :] = last
            for c in range(8):
                target = pl.multiple_of(i * (8 * rows) + c * rows, rows)
                same_ref[pl.ds(target, rows), :] = natural[
                    pl.ds(base + c * pitch + 8, rows), :
                ].astype(jnp.bfloat16)
                before_ref[pl.ds(target, rows), :] = natural[
                    pl.ds(base + c * pitch + 7, rows), :
                ].astype(jnp.bfloat16)
            return 0

        lax.fori_loop(0, chan_count // 8, pack, 0)

        lane = lax.broadcasted_iota(jnp.int32, (rows, LANES), 1)
        lane_half = lane.astype(jnp.float32).astype(jnp.bfloat16)
        row_lane = lax.broadcasted_iota(jnp.int32, (1, LANES), 1)
        sign = (1 - 2 * (lax.broadcasted_iota(jnp.int32, (padded_rows, LANES), 1) % 2)).astype(jnp.float32)
        apart = (
            lax.broadcasted_iota(jnp.int32, (padded_rows, width), 0)
            - lax.broadcasted_iota(jnp.int32, (padded_rows, width), 1) % rows
        ).astype(jnp.float32)

        def piece(k, j):
            target = lax.rem(me + 1 + k, tm_count)
            return pltpu.make_async_remote_copy(
                src_ref=part_ref.at[target],
                dst_ref=held_ref.at[band, me],
                send_sem=sent.at[k, j],
                recv_sem=arrived.at[k, j],
                device_id={"tm": target, "band": lax.rem(band + j, band_count)},
                device_id_type=mesh_ids,
            )

        def one_dm(k, _):
            dm = lax.rem(me + 1 + k, tm_count)

            def one_block(n, total):
                @pl.when((n == 1) & (k == 1))
                def _():
                    pl.semaphore_wait(barrier, peers)

                @pl.when((n == 1) & (k > 0))
                def _():
                    for j in range(band_count):
                        piece(k - 1, j).start()

                for b in range(block // group):
                    turned = []
                    for i in range(group):
                        chan = n * block + b * group + i
                        low = delay_ref[dm, chan] & (LANES - 1)
                        start = pl.multiple_of(chan * rows, rows)
                        edge = jnp.full((rows, LANES), (LANES - low).astype(jnp.float32)).astype(jnp.bfloat16)
                        merged = jnp.where(
                            lane_half < edge,
                            same_ref[pl.ds(start, rows), :],
                            before_ref[pl.ds(start, rows), :],
                        )
                        rolled = pltpu.roll(merged, low, 1)
                        top = rolled[:16].astype(jnp.float32)[:1]
                        carry_ref[pl.ds(chan, 1), :] = jnp.where(row_lane < low, top, 0.0)
                        turned.append(rolled)
                    place_in = pl.multiple_of(
                        lax.rem(n * block + b * group, LANES) * rows, width
                    )
                    lags = lag_rows[(n * block) // LANES, pl.ds(dm, 1), pl.ds(place_in, width)]
                    chosen = (apart == lags).astype(jnp.float32).astype(jnp.bfloat16)
                    total = total + jnp.dot(
                        chosen, jnp.concatenate(turned, axis=0), preferred_element_type=jnp.float32
                    )
                return total

            total = lax.fori_loop(
                0, chan_count // block, one_block, jnp.zeros((padded_rows, LANES), jnp.float32)
            )
            row = lax.broadcasted_iota(jnp.int32, (padded_rows, chan_count), 0)
            lags = lag_ref[pl.ds(dm, 1), :] >> lane_bits
            fix = (row == lags + rows).astype(jnp.float32) - (row == lags).astype(jnp.float32)
            total = total + jnp.dot(
                fix.astype(jnp.bfloat16),
                carry_ref[...].astype(jnp.bfloat16),
                preferred_element_type=jnp.float32,
            )
            half_rate = jnp.sum(total * sign) * sign * (1.0 / padded_len)
            result = ((total - half_rate) * scale).astype(jnp.bfloat16)
            part_ref[dm] = result

            @pl.when(k == dm_count - 1)
            def _():
                held_ref[band, me] = result

            return 0

        lax.fori_loop(0, dm_count, one_dm, 0)

        own = dm_count - 1
        for j in range(1, band_count):
            piece(own, j).start()
        for k in range(own):
            for j in range(band_count):
                piece(k, j).wait()
        for j in range(1, band_count):
            piece(own, j).wait()

        tail = jnp.zeros((rows, LANES), jnp.float32)
        for s in range(tm_count):
            piece_sum = held_ref[0, s].astype(jnp.float32)
            for b in range(1, band_count):
                piece_sum = piece_sum + held_ref[b, s].astype(jnp.float32)
            out_ref[s * rows : (s + 1) * rows, :] = piece_sum[:rows] + tail
            tail = piece_sum[rows:]

    vmem = pl.BlockSpec(memory_space=pltpu.VMEM)
    return pl.pallas_call(
        kernel,
        out_shape=jax.ShapeDtypeStruct((tm_count * rows, LANES), jnp.float32),
        in_specs=[
            pl.BlockSpec(memory_space=pltpu.SMEM),
            vmem,
            pl.BlockSpec(memory_space=pl.ANY),
            vmem,
        ],
        out_specs=vmem,
        scratch_shapes=[
            pltpu.VMEM((chan_count, slab_len), jnp.bfloat16),
            pltpu.VMEM((chan_count * pitch, LANES), jnp.float32),
            pltpu.VMEM((chan_count * rows, LANES), jnp.bfloat16),
            pltpu.VMEM((chan_count * rows, LANES), jnp.bfloat16),
            pltpu.VMEM((chan_count, rows), jnp.bfloat16),
            pltpu.VMEM((spans, dm_count, rows * LANES), jnp.float32),
            pltpu.VMEM((chan_count, LANES), jnp.float32),
            pltpu.VMEM((dm_count, padded_rows, LANES), jnp.bfloat16),
            pltpu.VMEM((band_count, tm_count, padded_rows, LANES), jnp.bfloat16),
            pltpu.SemaphoreType.DMA((chunks,)),
            pltpu.SemaphoreType.DMA((dm_count, band_count)),
            pltpu.SemaphoreType.DMA((dm_count, band_count)),
        ],
        compiler_params=pltpu.CompilerParams(
            collective_id=0, has_side_effects=True, vmem_limit_bytes=56 << 20
        ),
    )(delays, delays, samples, clip_mask.T)


def correlate(framed, templates, bin_count):
    tmpl_count, tap_len = templates.shape[1:]
    blocks = tap_len // LANES
    frame_len = framed.shape[1]
    width = 1024
    steps = bin_count // width

    def kernel(framed_ref, tmpl_ref, out_ref, taps_ref, shifted_ref):
        step = pl.program_id(0)

        @pl.when(step == 0)
        def _():
            row = lax.broadcasted_iota(jnp.int32, (LANES, LANES), 0)
            col = lax.broadcasted_iota(jnp.int32, (LANES, LANES), 1)
            flip = (row + col == LANES - 1).astype(jnp.bfloat16)
            for b in range(blocks):
                cut = slice(b * LANES, (b + 1) * LANES)
                real = jnp.dot(tmpl_ref[0, :, cut], flip, preferred_element_type=jnp.float32)
                imag = jnp.dot(tmpl_ref[1, :, cut], flip, preferred_element_type=jnp.float32)
                taps_ref[b, :tmpl_count, :LANES] = real.astype(jnp.bfloat16)
                taps_ref[b, :tmpl_count, LANES:] = (-imag).astype(jnp.bfloat16)
                taps_ref[b, tmpl_count:, :LANES] = imag.astype(jnp.bfloat16)
                taps_ref[b, tmpl_count:, LANES:] = real.astype(jnp.bfloat16)
            for part in range(2):
                spread = jnp.broadcast_to(framed_ref[part : part + 1, :], (8, frame_len))
                base = pltpu.roll(spread, 0, 1, stride=1, stride_axis=0)
                for g in range(LANES // 16):
                    lower = base if g == 0 else pltpu.roll(base, 16 * g, 1)
                    upper = pltpu.roll(base, 16 * g + 8, 1)
                    start = part * LANES + 16 * g
                    shifted_ref[start : start + 16, :] = jnp.concatenate(
                        [lower, upper], axis=0
                    ).astype(jnp.bfloat16)

        total = jnp.zeros((2 * tmpl_count, width), jnp.float32)
        for b in range(blocks):
            first = pl.multiple_of(step * width + (b + 1) * LANES, LANES)
            total = total + jnp.dot(
                taps_ref[b], shifted_ref[:, pl.ds(first, width)], preferred_element_type=jnp.float32
            )
        out_ref[0] = jnp.square(total[:tmpl_count]) + jnp.square(total[tmpl_count:])

    return pl.pallas_call(
        kernel,
        out_shape=jax.ShapeDtypeStruct((1, tmpl_count, bin_count), jnp.float32),
        grid=(steps,),
        in_specs=[
            pl.BlockSpec((2, frame_len), lambda i: (0, 0)),
            pl.BlockSpec(templates.shape, lambda i: (0, 0, 0)),
        ],
        out_specs=pl.BlockSpec((1, tmpl_count, width), lambda i: (0, 0, i)),
        scratch_shapes=[
            pltpu.VMEM((blocks, 2 * tmpl_count, 2 * LANES), jnp.bfloat16),
            pltpu.VMEM((2 * LANES, frame_len), jnp.bfloat16),
        ],
        compiler_params=pltpu.CompilerParams(vmem_limit_bytes=48 << 20),
    )(framed, templates)


def local(samples, clip_mask, delays, templates):
    return search(dedisperse(samples, clip_mask, delays), templates)


def search(whole, templates):
    row_count, inner_len = whole.shape
    total_len = row_count * inner_len
    bin_cols = SEARCH // row_count
    scale_bins = 1.0 / math.sqrt(total_len)
    outer_cos, outer_sin = phase_table(counting(row_count), counting(row_count), row_count)
    table_outer = jnp.concatenate([outer_cos, -outer_sin], axis=0)
    hold_cos, hold_sin = phase_table(counting(row_count), counting(inner_len), total_len)
    own_cols = bin_cols // lax.axis_size("band")
    folded = jnp.dot(table_outer, whole, precision=fine)
    fold_real = folded[:row_count]
    fold_imag = folded[row_count:]
    hold_real = fold_real * hold_cos + fold_imag * hold_sin
    hold_imag = fold_imag * hold_cos - fold_real * hold_sin
    half_taps = templates.shape[2] // 2
    side_cols = -(-half_taps // row_count)
    cols = lax.axis_index("band") * own_cols - side_cols + counting(own_cols + 2 * side_cols)
    last_cos, last_sin = phase_table(counting(inner_len), cols % inner_len, inner_len)
    inside = ((cols >= 0) & (cols < bin_cols)).astype(jnp.float32) * scale_bins
    last_cos = last_cos * inside
    last_sin = last_sin * inside
    table_last = jnp.concatenate(
        [
            jnp.concatenate([last_cos, -last_sin], axis=1),
            jnp.concatenate([last_sin, last_cos], axis=1),
        ],
        axis=0,
    )
    out = jnp.dot(jnp.concatenate([hold_real, hold_imag], axis=1), table_last, precision=fine)
    ordered = out.T.reshape(2, -1)
    local_bins = own_cols * row_count
    skip = side_cols * row_count - half_taps
    if skip:
        framed = ordered[:, skip - 1 : skip - 1 + local_bins + 2 * half_taps]
    else:
        framed = jnp.pad(ordered[:, :-1], ((0, 0), (1, 0)))
    return correlate(framed, templates, local_bins)


def solution(mesh):
    in_specs = (P(("beam", "band"), "tm"), P(("beam", "band"), "tm"), P(None, "band"), P())
    out_specs = P(("beam", "tm"), None, "band")
    return jax.shard_map(local, mesh=mesh, in_specs=in_specs, out_specs=out_specs, check_vma=False)
```

```python
import math

import jax
import jax.numpy as jnp
from jax import lax
from jax.experimental import pallas as pl
from jax.experimental.pallas import tpu as pltpu
from jax.sharding import PartitionSpec as P

CHANNELS = 1024
SEARCH = 16384
LANES = 128

clip_level = 2.5
fine = lax.Precision.HIGH


def counting(length):
    return jnp.arange(length, dtype=jnp.int32)


def phase_table(first_index, second_index, period):
    turn_count = first_index[:, None] * second_index[None, :] % period
    angles = turn_count.astype(jnp.float32) * (2.0 * math.pi / period)
    return (jnp.cos(angles), jnp.sin(angles))


def dedisperse(samples, clip_mask, delays):
    chan_count, slab_len = samples.shape
    rows = slab_len // LANES
    dm_count = delays.shape[0]
    tm_count = lax.axis_size("tm")
    band_count = lax.axis_size("band")
    padded_len = 2 * slab_len
    scale = 1.0 / math.sqrt(CHANNELS)
    assert clip_mask.shape[1] == rows and dm_count == tm_count
    mesh_ids = pl.DeviceIdType.MESH
    lane_bits = LANES.bit_length() - 1
    pitch = rows + 8
    width = 2 * LANES
    chunks = slab_len // width
    group = width // rows
    held_back = min(8, chan_count // group - 1)
    spans = chan_count // LANES
    padded_rows = 2 * rows

    def kernel(
        delay_ref, lag_ref, sample_ref, mask_ref, out_ref,
        held_in, natural, same_ref, before_ref, flag_ref, lag_rows, carry_ref, part_ref, held_ref,
        load_sem, sent, arrived,
    ):
        me = lax.axis_index("tm")
        band = lax.axis_index("band")

        def load(j):
            start = pl.multiple_of(j * width, width)
            cut = pl.ds(start, width)
            return pltpu.make_async_copy(sample_ref.at[:, cut], held_in.at[:, cut], load_sem.at[j])

        for j in range(chunks):
            load(j).start()

        barrier = pltpu.get_barrier_semaphore()
        peers = tm_count * band_count - 1
        place = me * band_count + band

        def greet(k, _):
            other = lax.rem(place + k, peers + 1)
            pl.semaphore_signal(
                barrier, 1,
                device_id={"tm": other // band_count, "band": lax.rem(other, band_count)},
                device_id_type=mesh_ids,
            )
            return 0

        lax.fori_loop(1, peers + 1, greet, 0)

        flag_ref[...] = mask_ref[...].astype(jnp.float32).T.astype(jnp.bfloat16)
        spread_lane = lax.broadcasted_iota(jnp.int32, (LANES, rows * LANES), 1)
        spread_row = lax.broadcasted_iota(jnp.int32, (LANES, rows * LANES), 0)
        spread = (spread_lane // rows == spread_row).astype(jnp.float32).astype(jnp.bfloat16)
        row_lags = (lag_ref[...] >> lane_bits).astype(jnp.float32).astype(jnp.bfloat16)
        for i in range(spans):
            lag_rows[i] = jnp.dot(
                row_lags[:, i * LANES : (i + 1) * LANES], spread, preferred_element_type=jnp.float32
            )

        def take(j, _):
            load(j).wait()
            start = pl.multiple_of(j * width, width)
            first = lax.broadcasted_iota(jnp.int32, (rows, width), 0) - 2 * j
            which = lax.broadcasted_iota(jnp.int32, (rows, width), 1) // LANES
            pick = (first == which).astype(jnp.float32).astype(jnp.bfloat16)
            flags = jnp.dot(flag_ref[...], pick, preferred_element_type=jnp.float32)
            for g in range(chan_count // 16):
                values = held_in[16 * g : 16 * g + 16, pl.ds(start, width)]
                values = jnp.clip(values, -clip_level, clip_level).astype(jnp.float32)
                values = values * flags[16 * g : 16 * g + 16]
                for h in range(2):
                    for t in range(2):
                        natural[pl.ds((16 * g + 8 * t) * pitch + 8 + 2 * j + h, 8, stride=pitch), :] = (
                            values[8 * t : 8 * t + 8, h * LANES : (h + 1) * LANES]
                        )
            return 0

        lax.fori_loop(0, chunks, take, 0)

        def pack(i, _):
            base = pl.multiple_of(i * (8 * pitch), 8)
            last = natural[pl.ds(base + pitch - 1, 8, stride=pitch), :]
            natural[pl.ds(base + 7, 8, stride=pitch), :] = last
            for c in range(8):
                target = pl.multiple_of(i * (8 * rows) + c * rows, rows)
                same_ref[pl.ds(target, rows), :] = natural[
                    pl.ds(base + c * pitch + 8, rows), :
                ].astype(jnp.bfloat16)
                before_ref[pl.ds(target, rows), :] = natural[
                    pl.ds(base + c * pitch + 7, rows), :
                ].astype(jnp.bfloat16)
            return 0

        lax.fori_loop(0, chan_count // 8, pack, 0)

        lane = lax.broadcasted_iota(jnp.int32, (rows, LANES), 1)
        from_end = (LANES - 1 - lane).astype(jnp.float32).astype(jnp.bfloat16)
        row_lane = lax.broadcasted_iota(jnp.int32, (1, LANES), 1).astype(jnp.float32)
        sign = (1 - 2 * (lax.broadcasted_iota(jnp.int32, (padded_rows, LANES), 1) % 2)).astype(jnp.float32)
        apart = (
            lax.broadcasted_iota(jnp.int32, (padded_rows, width), 0)
            - lax.broadcasted_iota(jnp.int32, (padded_rows, width), 1) % rows
        ).astype(jnp.float32)

        def piece(k, j):
            target = lax.rem(me + 1 + k, tm_count)
            return pltpu.make_async_remote_copy(
                src_ref=part_ref.at[target],
                dst_ref=held_ref.at[band, me],
                send_sem=sent.at[k, j],
                recv_sem=arrived.at[k, j],
                device_id={"tm": target, "band": lax.rem(band + j, band_count)},
                device_id_type=mesh_ids,
            )

        def one_dm(k, _):
            dm = lax.rem(me + 1 + k, tm_count)

            total = jnp.zeros((padded_rows, LANES), jnp.float32)
            for n in range(chan_count // group):
                if n == held_back:

                    @pl.when(k == 1)
                    def _():
                        pl.semaphore_wait(barrier, peers)

                    @pl.when(k > 0)
                    def _():
                        for j in range(band_count):
                            piece(k - 1, j).start()

                turned = []
                for chan in range(n * group, (n + 1) * group):
                    low = delay_ref[dm, chan] & (LANES - 1)
                    low_float = low.astype(jnp.float32)
                    cut = slice(chan * rows, (chan + 1) * rows)
                    merged = jnp.where(
                        from_end >= jnp.full((rows, LANES), low_float).astype(jnp.bfloat16),
                        same_ref[cut],
                        before_ref[cut],
                    )
                    rolled = pltpu.roll(merged, low, 1)
                    top = rolled[:16].astype(jnp.float32)[:1]
                    carry_ref[chan : chan + 1, :] = jnp.where(row_lane < low_float, top, 0.0)
                    turned.append(rolled)
                first = n * group % LANES * rows
                lags = lag_rows[n * group // LANES, pl.ds(dm, 1), first : first + width]
                chosen = (apart == lags).astype(jnp.float32).astype(jnp.bfloat16)
                total = total + jnp.dot(
                    chosen, jnp.concatenate(turned, axis=0), preferred_element_type=jnp.float32
                )

            row = lax.broadcasted_iota(jnp.int32, (padded_rows, chan_count), 0)
            lags = lag_ref[pl.ds(dm, 1), :] >> lane_bits
            fix = (row == lags + rows).astype(jnp.float32) - (row == lags).astype(jnp.float32)
            total = total + jnp.dot(
                fix.astype(jnp.bfloat16),
                carry_ref[...].astype(jnp.bfloat16),
                preferred_element_type=jnp.float32,
            )
            half_rate = jnp.sum(total * sign) * sign * (1.0 / padded_len)
            result = ((total - half_rate) * scale).astype(jnp.bfloat16)
            part_ref[dm] = result

            @pl.when(k == dm_count - 1)
            def _():
                held_ref[band, me] = result

            return 0

        lax.fori_loop(0, dm_count, one_dm, 0)

        own = dm_count - 1
        for j in range(1, band_count):
            piece(own, j).start()
        for k in range(own):
            for j in range(band_count):
                piece(k, j).wait()
        for j in range(1, band_count):
            piece(own, j).wait()

        tail = jnp.zeros((rows, LANES), jnp.float32)
        for s in range(tm_count):
            piece_sum = held_ref[0, s].astype(jnp.float32)
            for b in range(1, band_count):
                piece_sum = piece_sum + held_ref[b, s].astype(jnp.float32)
            out_ref[s * rows : (s + 1) * rows, :] = piece_sum[:rows] + tail
            tail = piece_sum[rows:]

    vmem = pl.BlockSpec(memory_space=pltpu.VMEM)
    return pl.pallas_call(
        kernel,
        out_shape=jax.ShapeDtypeStruct((tm_count * rows, LANES), jnp.float32),
        in_specs=[
            pl.BlockSpec(memory_space=pltpu.SMEM),
            vmem,
            pl.BlockSpec(memory_space=pl.ANY),
            vmem,
        ],
        out_specs=vmem,
        scratch_shapes=[
            pltpu.VMEM((chan_count, slab_len), jnp.bfloat16),
            pltpu.VMEM((chan_count * pitch, LANES), jnp.float32),
            pltpu.VMEM((chan_count * rows, LANES), jnp.bfloat16),
            pltpu.VMEM((chan_count * rows, LANES), jnp.bfloat16),
            pltpu.VMEM((chan_count, rows), jnp.bfloat16),
            pltpu.VMEM((spans, dm_count, rows * LANES), jnp.float32),
            pltpu.VMEM((chan_count, LANES), jnp.float32),
            pltpu.VMEM((dm_count, padded_rows, LANES), jnp.bfloat16),
            pltpu.VMEM((band_count, tm_count, padded_rows, LANES), jnp.bfloat16),
            pltpu.SemaphoreType.DMA((chunks,)),
            pltpu.SemaphoreType.DMA((dm_count, band_count)),
            pltpu.SemaphoreType.DMA((dm_count, band_count)),
        ],
        compiler_params=pltpu.CompilerParams(
            collective_id=0, has_side_effects=True, vmem_limit_bytes=56 << 20
        ),
    )(delays, delays, samples, clip_mask.T)


def correlate(framed, templates, bin_count):
    tmpl_count, tap_len = templates.shape[1:]
    blocks = tap_len // LANES
    frame_len = framed.shape[1]
    width = 1024
    steps = bin_count // width

    def kernel(framed_ref, tmpl_ref, out_ref, taps_ref, shifted_ref):
        step = pl.program_id(0)

        @pl.when(step == 0)
        def _():
            row = lax.broadcasted_iota(jnp.int32, (LANES, LANES), 0)
            col = lax.broadcasted_iota(jnp.int32, (LANES, LANES), 1)
            flip = (row + col == LANES - 1).astype(jnp.bfloat16)
            for b in range(blocks):
                cut = slice(b * LANES, (b + 1) * LANES)
                real = jnp.dot(tmpl_ref[0, :, cut], flip, preferred_element_type=jnp.float32)
                imag = jnp.dot(tmpl_ref[1, :, cut], flip, preferred_element_type=jnp.float32)
                taps_ref[b, :tmpl_count, :LANES] = real.astype(jnp.bfloat16)
                taps_ref[b, :tmpl_count, LANES:] = (-imag).astype(jnp.bfloat16)
                taps_ref[b, tmpl_count:, :LANES] = imag.astype(jnp.bfloat16)
                taps_ref[b, tmpl_count:, LANES:] = real.astype(jnp.bfloat16)
            for part in range(2):
                spread = jnp.broadcast_to(framed_ref[part : part + 1, :], (8, frame_len))
                base = pltpu.roll(spread, 0, 1, stride=1, stride_axis=0)
                for g in range(LANES // 16):
                    lower = base if g == 0 else pltpu.roll(base, 16 * g, 1)
                    upper = pltpu.roll(base, 16 * g + 8, 1)
                    start = part * LANES + 16 * g
                    shifted_ref[start : start + 16, :] = jnp.concatenate(
                        [lower, upper], axis=0
                    ).astype(jnp.bfloat16)

        total = jnp.zeros((2 * tmpl_count, width), jnp.float32)
        for b in range(blocks):
            first = pl.multiple_of(step * width + (b + 1) * LANES, LANES)
            total = total + jnp.dot(
                taps_ref[b], shifted_ref[:, pl.ds(first, width)], preferred_element_type=jnp.float32
            )
        out_ref[0] = jnp.square(total[:tmpl_count]) + jnp.square(total[tmpl_count:])

    return pl.pallas_call(
        kernel,
        out_shape=jax.ShapeDtypeStruct((1, tmpl_count, bin_count), jnp.float32),
        grid=(steps,),
        in_specs=[
            pl.BlockSpec((2, frame_len), lambda i: (0, 0)),
            pl.BlockSpec(templates.shape, lambda i: (0, 0, 0)),
        ],
        out_specs=pl.BlockSpec((1, tmpl_count, width), lambda i: (0, 0, i)),
        scratch_shapes=[
            pltpu.VMEM((blocks, 2 * tmpl_count, 2 * LANES), jnp.bfloat16),
            pltpu.VMEM((2 * LANES, frame_len), jnp.bfloat16),
        ],
        compiler_params=pltpu.CompilerParams(vmem_limit_bytes=48 << 20),
    )(framed, templates)


def local(samples, clip_mask, delays, templates):
    return search(dedisperse(samples, clip_mask, delays), templates)


def search(whole, templates):
    row_count, inner_len = whole.shape
    total_len = row_count * inner_len
    bin_cols = SEARCH // row_count
    scale_bins = 1.0 / math.sqrt(total_len)
    outer_cos, outer_sin = phase_table(counting(row_count), counting(row_count), row_count)
    table_outer = jnp.concatenate([outer_cos, -outer_sin], axis=0)
    hold_cos, hold_sin = phase_table(counting(row_count), counting(inner_len), total_len)
    own_cols = bin_cols // lax.axis_size("band")
    folded = jnp.dot(table_outer, whole, precision=fine)
    fold_real = folded[:row_count]
    fold_imag = folded[row_count:]
    hold_real = fold_real * hold_cos + fold_imag * hold_sin
    hold_imag = fold_imag * hold_cos - fold_real * hold_sin
    half_taps = templates.shape[2] // 2
    side_cols = -(-half_taps // row_count)
    cols = lax.axis_index("band") * own_cols - side_cols + counting(own_cols + 2 * side_cols)
    last_cos, last_sin = phase_table(counting(inner_len), cols % inner_len, inner_len)
    inside = ((cols >= 0) & (cols < bin_cols)).astype(jnp.float32) * scale_bins
    last_cos = last_cos * inside
    last_sin = last_sin * inside
    table_last = jnp.concatenate(
        [
            jnp.concatenate([last_cos, -last_sin], axis=1),
            jnp.concatenate([last_sin, last_cos], axis=1),
        ],
        axis=0,
    )
    out = jnp.dot(jnp.concatenate([hold_real, hold_imag], axis=1), table_last, precision=fine)
    ordered = out.T.reshape(2, -1)
    local_bins = own_cols * row_count
    skip = side_cols * row_count - half_taps
    if skip:
        framed = ordered[:, skip - 1 : skip - 1 + local_bins + 2 * half_taps]
    else:
        framed = jnp.pad(ordered[:, :-1], ((0, 0), (1, 0)))
    return correlate(framed, templates, local_bins)


def solution(mesh):
    in_specs = (P(("beam", "band"), "tm"), P(("beam", "band"), "tm"), P(None, "band"), P())
    out_specs = P(("beam", "tm"), None, "band")
    return jax.shard_map(local, mesh=mesh, in_specs=in_specs, out_specs=out_specs, check_vma=False)
```

```python
import math

import jax
import jax.numpy as jnp
import numpy as np
from jax import lax
from jax.experimental import pallas as pl
from jax.experimental.pallas import tpu as pltpu
from jax.sharding import PartitionSpec as P

CHANNELS = 1024
SEARCH = 16384
LANES = 128

clip_level = 2.5


def dedisperse(samples, clip_mask, delays):
    chan_count, slab_len = samples.shape
    rows = slab_len // LANES
    dm_count = delays.shape[0]
    tm_count = lax.axis_size("tm")
    band_count = lax.axis_size("band")
    padded_len = 2 * slab_len
    scale = 1.0 / math.sqrt(CHANNELS)
    assert clip_mask.shape[1] == rows and dm_count == tm_count
    mesh_ids = pl.DeviceIdType.MESH
    lane_bits = LANES.bit_length() - 1
    pitch = rows + 8
    width = 2 * LANES
    chunks = slab_len // width
    group = width // rows
    held_back = min(8, chan_count // group - 1)
    spans = chan_count // LANES
    padded_rows = 2 * rows

    def kernel(
        delay_ref, lag_ref, sample_ref, mask_ref, out_ref,
        held_in, natural, same_ref, before_ref, flag_ref, lag_rows, carry_ref, part_ref, held_ref,
        load_sem, sent, arrived,
    ):
        me = lax.axis_index("tm")
        band = lax.axis_index("band")

        def load(j):
            start = pl.multiple_of(j * width, width)
            cut = pl.ds(start, width)
            return pltpu.make_async_copy(sample_ref.at[:, cut], held_in.at[:, cut], load_sem.at[j])

        for j in range(chunks):
            load(j).start()

        barrier = pltpu.get_barrier_semaphore()
        peers = tm_count * band_count - 1
        place = me * band_count + band

        def greet(k, _):
            other = lax.rem(place + k, peers + 1)
            pl.semaphore_signal(
                barrier, 1,
                device_id={"tm": other // band_count, "band": lax.rem(other, band_count)},
                device_id_type=mesh_ids,
            )
            return 0

        lax.fori_loop(1, peers + 1, greet, 0)

        flag_ref[...] = mask_ref[...].astype(jnp.float32).T.astype(jnp.bfloat16)
        spread_lane = lax.broadcasted_iota(jnp.int32, (LANES, rows * LANES), 1)
        spread_row = lax.broadcasted_iota(jnp.int32, (LANES, rows * LANES), 0)
        spread = (spread_lane // rows == spread_row).astype(jnp.float32).astype(jnp.bfloat16)
        row_lags = (lag_ref[...] >> lane_bits).astype(jnp.float32).astype(jnp.bfloat16)
        for i in range(spans):
            lag_rows[i] = jnp.dot(
                row_lags[:, i * LANES : (i + 1) * LANES], spread, preferred_element_type=jnp.float32
            )

        def take(j, _):
            load(j).wait()
            start = pl.multiple_of(j * width, width)
            first = lax.broadcasted_iota(jnp.int32, (rows, width), 0) - 2 * j
            which = lax.broadcasted_iota(jnp.int32, (rows, width), 1) // LANES
            pick = (first == which).astype(jnp.float32).astype(jnp.bfloat16)
            flags = jnp.dot(flag_ref[...], pick, preferred_element_type=jnp.float32)
            for g in range(chan_count // 16):
                values = held_in[16 * g : 16 * g + 16, pl.ds(start, width)]
                values = jnp.clip(values, -clip_level, clip_level).astype(jnp.float32)
                values = values * flags[16 * g : 16 * g + 16]
                for h in range(2):
                    for t in range(2):
                        natural[pl.ds((16 * g + 8 * t) * pitch + 8 + 2 * j + h, 8, stride=pitch), :] = (
                            values[8 * t : 8 * t + 8, h * LANES : (h + 1) * LANES]
                        )
            return 0

        lax.fori_loop(0, chunks, take, 0)

        def pack(i, _):
            base = pl.multiple_of(i * (8 * pitch), 8)
            last = natural[pl.ds(base + pitch - 1, 8, stride=pitch), :]
            natural[pl.ds(base + 7, 8, stride=pitch), :] = last
            for c in range(8):
                target = pl.multiple_of(i * (8 * rows) + c * rows, rows)
                same_ref[pl.ds(target, rows), :] = natural[
                    pl.ds(base + c * pitch + 8, rows), :
                ].astype(jnp.bfloat16)
                before_ref[pl.ds(target, rows), :] = natural[
                    pl.ds(base + c * pitch + 7, rows), :
                ].astype(jnp.bfloat16)
            return 0

        lax.fori_loop(0, chan_count // 8, pack, 0)

        lane = lax.broadcasted_iota(jnp.int32, (rows, LANES), 1)
        from_end = (LANES - 1 - lane).astype(jnp.float32).astype(jnp.bfloat16)
        row_lane = lax.broadcasted_iota(jnp.int32, (1, LANES), 1).astype(jnp.float32)
        sign = (1 - 2 * (lax.broadcasted_iota(jnp.int32, (padded_rows, LANES), 1) % 2)).astype(jnp.float32)
        apart = (
            lax.broadcasted_iota(jnp.int32, (padded_rows, width), 0)
            - lax.broadcasted_iota(jnp.int32, (padded_rows, width), 1) % rows
        ).astype(jnp.float32)

        def piece(k, j):
            target = lax.rem(me + 1 + k, tm_count)
            return pltpu.make_async_remote_copy(
                src_ref=part_ref.at[target],
                dst_ref=held_ref.at[band, me],
                send_sem=sent.at[k, j],
                recv_sem=arrived.at[k, j],
                device_id={"tm": target, "band": lax.rem(band + j, band_count)},
                device_id_type=mesh_ids,
            )

        def one_dm(k, _):
            dm = lax.rem(me + 1 + k, tm_count)

            total = jnp.zeros((padded_rows, LANES), jnp.float32)
            for n in range(chan_count // group):
                if n == held_back:

                    @pl.when(k == 1)
                    def _():
                        pl.semaphore_wait(barrier, peers)

                    @pl.when(k > 0)
                    def _():
                        for j in range(band_count):
                            piece(k - 1, j).start()

                turned = []
                for chan in range(n * group, (n + 1) * group):
                    low = delay_ref[dm, chan] & (LANES - 1)
                    low_float = low.astype(jnp.float32)
                    cut = slice(chan * rows, (chan + 1) * rows)
                    merged = jnp.where(
                        from_end >= jnp.full((rows, LANES), low_float).astype(jnp.bfloat16),
                        same_ref[cut],
                        before_ref[cut],
                    )
                    rolled = pltpu.roll(merged, low, 1)
                    top = rolled[:16].astype(jnp.float32)[:1]
                    carry_ref[chan : chan + 1, :] = jnp.where(row_lane < low_float, top, 0.0)
                    turned.append(rolled)
                first = n * group % LANES * rows
                lags = lag_rows[n * group // LANES, pl.ds(dm, 1), first : first + width]
                chosen = (apart == lags).astype(jnp.float32).astype(jnp.bfloat16)
                total = total + jnp.dot(
                    chosen, jnp.concatenate(turned, axis=0), preferred_element_type=jnp.float32
                )

            row = lax.broadcasted_iota(jnp.int32, (padded_rows, chan_count), 0)
            lags = lag_ref[pl.ds(dm, 1), :] >> lane_bits
            fix = (row == lags + rows).astype(jnp.float32) - (row == lags).astype(jnp.float32)
            total = total + jnp.dot(
                fix.astype(jnp.bfloat16),
                carry_ref[...].astype(jnp.bfloat16),
                preferred_element_type=jnp.float32,
            )
            half_rate = jnp.sum(total * sign) * sign * (1.0 / padded_len)
            result = ((total - half_rate) * scale).astype(jnp.bfloat16)
            part_ref[dm] = result

            @pl.when(k == dm_count - 1)
            def _():
                held_ref[band, me] = result

            return 0

        lax.fori_loop(0, dm_count, one_dm, 0)

        own = dm_count - 1
        for j in range(1, band_count):
            piece(own, j).start()
        for k in range(own):
            for j in range(band_count):
                piece(k, j).wait()
        for j in range(1, band_count):
            piece(own, j).wait()

        tail = jnp.zeros((rows, LANES), jnp.float32)
        for s in range(tm_count):
            piece_sum = held_ref[0, s].astype(jnp.float32)
            for b in range(1, band_count):
                piece_sum = piece_sum + held_ref[b, s].astype(jnp.float32)
            out_ref[s * rows : (s + 1) * rows, :] = piece_sum[:rows] + tail
            tail = piece_sum[rows:]

    vmem = pl.BlockSpec(memory_space=pltpu.VMEM)
    return pl.pallas_call(
        kernel,
        out_shape=jax.ShapeDtypeStruct((tm_count * rows, LANES), jnp.float32),
        in_specs=[
            pl.BlockSpec(memory_space=pltpu.SMEM),
            vmem,
            pl.BlockSpec(memory_space=pl.ANY),
            vmem,
        ],
        out_specs=vmem,
        scratch_shapes=[
            pltpu.VMEM((chan_count, slab_len), jnp.bfloat16),
            pltpu.VMEM((chan_count * pitch, LANES), jnp.float32),
            pltpu.VMEM((chan_count * rows, LANES), jnp.bfloat16),
            pltpu.VMEM((chan_count * rows, LANES), jnp.bfloat16),
            pltpu.VMEM((chan_count, rows), jnp.bfloat16),
            pltpu.VMEM((spans, dm_count, rows * LANES), jnp.float32),
            pltpu.VMEM((chan_count, LANES), jnp.float32),
            pltpu.VMEM((dm_count, padded_rows, LANES), jnp.bfloat16),
            pltpu.VMEM((band_count, tm_count, padded_rows, LANES), jnp.bfloat16),
            pltpu.SemaphoreType.DMA((chunks,)),
            pltpu.SemaphoreType.DMA((dm_count, band_count)),
            pltpu.SemaphoreType.DMA((dm_count, band_count)),
        ],
        compiler_params=pltpu.CompilerParams(
            collective_id=0, has_side_effects=True, vmem_limit_bytes=54 << 20
        ),
    )(delays, delays, samples, clip_mask.T)


def halves(table):
    high = table.astype(jnp.bfloat16)
    low = (table - high.astype(np.float64)).astype(jnp.bfloat16)
    return np.stack([high, low])


def split(values):
    high = values.astype(jnp.bfloat16)
    return high, (values - high.astype(jnp.float32)).astype(jnp.bfloat16)


def three_pass(left, right, dims):
    def product(x, y):
        return lax.dot_general(x, y, (dims, ((), ())), preferred_element_type=jnp.float32)

    return product(left[0], right[1]) + product(left[1], right[0]) + product(left[0], right[0])


def turn(first_index, second_index, period):
    return (first_index[:, None] * second_index[None, :] % period) * (2.0 * math.pi / period)


def search(whole, templates):
    row_count, inner_len = whole.shape
    total_len = row_count * inner_len
    bin_cols = SEARCH // row_count
    band_count = lax.axis_size("band")
    own_cols = bin_cols // band_count
    tmpl_count, tap_len = templates.shape[1:]
    half_taps = tap_len // 2
    side_cols = -(-half_taps // row_count)
    col_count = own_cols + 2 * side_cols
    skip = side_cols * row_count - half_taps
    bin_count = own_cols * row_count
    frame_len = bin_count + tap_len
    blocks = tap_len // LANES
    width = 1024
    steps = bin_count // width
    assert skip % LANES == 0

    counts = np.arange(row_count)
    inner = np.arange(inner_len)
    outer = turn(counts, counts, row_count)
    outer_table = halves(np.concatenate([np.cos(outer), -np.sin(outer)], axis=0))
    hold = turn(counts, inner, total_len)
    hold_table = np.stack([np.cos(hold), np.sin(hold)]).astype(np.float32)
    last_tables = []
    for b in range(band_count):
        cols = b * own_cols - side_cols + np.arange(col_count)
        angles = turn(cols % inner_len, inner, inner_len)
        kept = ((cols >= 0) & (cols < bin_cols))[:, None] / math.sqrt(total_len)
        cosine, sine = np.cos(angles) * kept, np.sin(angles) * kept
        last_tables.append(
            halves(
                np.concatenate(
                    [
                        np.concatenate([cosine, sine], axis=1),
                        np.concatenate([-sine, cosine], axis=1),
                    ],
                    axis=0,
                )
            )
        )
    last_table = np.stack(last_tables)

    def kernel(whole_ref, outer_ref, hold_ref, last_ref, tmpl_ref, out_ref, framed_ref, taps_ref, shifted_ref):
        step = pl.program_id(0)

        @pl.when(step == 0)
        def _():
            row = lax.broadcasted_iota(jnp.int32, (LANES, LANES), 0)
            col = lax.broadcasted_iota(jnp.int32, (LANES, LANES), 1)
            flip = (row + col == LANES - 1).astype(jnp.bfloat16)
            for b in range(blocks):
                cut = slice(b * LANES, (b + 1) * LANES)
                real = jnp.dot(tmpl_ref[0, :, cut], flip, preferred_element_type=jnp.float32)
                imag = jnp.dot(tmpl_ref[1, :, cut], flip, preferred_element_type=jnp.float32)
                taps_ref[b, :tmpl_count, :LANES] = real.astype(jnp.bfloat16)
                taps_ref[b, :tmpl_count, LANES:] = (-imag).astype(jnp.bfloat16)
                taps_ref[b, tmpl_count:, :LANES] = imag.astype(jnp.bfloat16)
                taps_ref[b, tmpl_count:, LANES:] = real.astype(jnp.bfloat16)
            folded = three_pass((outer_ref[0], outer_ref[1]), split(whole_ref[...]), ((1,), (0,)))
            fold_real, fold_imag = folded[:row_count], folded[row_count:]
            hold_cos, hold_sin = hold_ref[0], hold_ref[1]
            held = jnp.concatenate(
                [fold_real * hold_cos + fold_imag * hold_sin, fold_imag * hold_cos - fold_real * hold_sin],
                axis=1,
            )
            band = lax.axis_index("band")
            bins = three_pass((last_ref[band, 0], last_ref[band, 1]), split(held), ((1,), (1,)))
            for part in range(2):
                for i in range(col_count):
                    framed_ref[part : part + 1, i * row_count : (i + 1) * row_count] = bins[
                        part * col_count + i : part * col_count + i + 1
                    ]
            for part in range(2):
                spread = jnp.broadcast_to(
                    framed_ref[part : part + 1, skip : skip + frame_len], (8, frame_len)
                )
                base = pltpu.roll(spread, 1, 1, stride=1, stride_axis=0)
                for g in range(LANES // 16):
                    lower = base if g == 0 else pltpu.roll(base, 16 * g, 1)
                    upper = pltpu.roll(base, 16 * g + 8, 1)
                    start = part * LANES + 16 * g
                    shifted_ref[start : start + 16, :] = jnp.concatenate(
                        [lower, upper], axis=0
                    ).astype(jnp.bfloat16)

        total = jnp.zeros((2 * tmpl_count, width), jnp.float32)
        for b in range(blocks):
            first = pl.multiple_of(step * width + (b + 1) * LANES, LANES)
            total = total + jnp.dot(
                taps_ref[b], shifted_ref[:, pl.ds(first, width)], preferred_element_type=jnp.float32
            )
        out_ref[0] = jnp.square(total[:tmpl_count]) + jnp.square(total[tmpl_count:])

    def resident(array):
        zeros = (0,) * array.ndim
        return pl.BlockSpec(array.shape, lambda i: zeros)

    operands = (whole, outer_table, hold_table, last_table, templates)
    return pl.pallas_call(
        kernel,
        out_shape=jax.ShapeDtypeStruct((1, tmpl_count, bin_count), jnp.float32),
        grid=(steps,),
        in_specs=[resident(x) for x in operands],
        out_specs=pl.BlockSpec((1, tmpl_count, width), lambda i: (0, 0, i)),
        scratch_shapes=[
            pltpu.VMEM((2, col_count * row_count), jnp.float32),
            pltpu.VMEM((blocks, 2 * tmpl_count, 2 * LANES), jnp.bfloat16),
            pltpu.VMEM((2 * LANES, frame_len), jnp.bfloat16),
        ],
        compiler_params=pltpu.CompilerParams(vmem_limit_bytes=48 << 20),
    )(*operands)


def local(samples, clip_mask, delays, templates):
    return search(dedisperse(samples, clip_mask, delays), templates)


def solution(mesh):
    in_specs = (P(("beam", "band"), "tm"), P(("beam", "band"), "tm"), P(None, "band"), P())
    out_specs = P(("beam", "tm"), None, "band")
    return jax.shard_map(local, mesh=mesh, in_specs=in_specs, out_specs=out_specs, check_vma=False)
```
